32 devices in a mesh: dp: 8 (over y, x, core), replica: 4 (over z).
Axes of the slice: x: 2, y: 2, z: 4, core: 2. Of those that a mesh axis runs over, the one named last changes fastest.
Arguments:
- gradient: bfloat16 [4, 8, 8, 8192], P('replica', 'dp'), may hold values from -6 to 6
- master: float32 [8, 8192], P('dp', 'replica'), may hold values from -0.0625 to 0.0625
- moment: float32 [8, 8192], P('dp', 'replica'), may hold values from -0.046875 to 0.046875
- second: float32 [8, 8192], P('dp', 'replica'), may hold values from 1e-06 to 0.0001
Outputs:
- new_params: bfloat16 [8, 8192], P('dp')
- new_master: float32 [8, 8192], P('dp', 'replica')
- new_moment: float32 [8, 8192], P('dp', 'replica')
- new_second: float32 [8, 8192], P('dp', 'replica')
- direction: float32 [8, 8192], P('dp', 'replica')
- ratios: float32 [4], replicated
The draws below stay inside these ranges and needn't reach their ends.
All inputs are finite; a program needn't handle non-finite values.
Results may differ from the reference program's by a relative error of at most 0.001.
Values may be sent and summed in bfloat16 or wider, within the bound.
A program may use at most 64 MiB of HBM per device.

```python
import math
import jax
import jax.numpy as jnp
from jax import lax

D = 8192
MATS = 4
STEP = 2
ROWS = 8
N_DP = 8
N_REPLICA = 4


def with_spikes(array, rng, source, target, parts, factor):
    def block_of(dim):
        return (jnp.arange(array.shape[dim]) // (array.shape[dim] // parts)).reshape((-1,) + (1,) * (array.ndim - 1 - dim))

    first = jax.random.permutation(rng, parts)[block_of(target)]
    far = (block_of(target) + parts // 2) % parts
    return jnp.where((block_of(source) == first) | (block_of(source) == far), factor * array, array)


def block_levels(stream_key, shape, split, low, high):
    loudness, own = 1.0, jax.random.fold_in(stream_key, 6)
    for position, parts in split:
        draws = jnp.exp(jax.random.uniform(jax.random.fold_in(own, position), (parts,), jnp.float32, low / len(split), high / len(split)))
        loudness = loudness * jnp.repeat(draws, shape[position] // parts).reshape([-1 if axis == position else 1 for axis in range(len(shape))])
    return loudness


def noise(own_key, dims, width, limit, cuts=(), kind=jnp.bfloat16):
    result = jax.random.normal(own_key, dims, jnp.float32) * width
    if len(cuts) > 0:
        result = block_levels(own_key, dims, cuts, -0.22, 0.18) * result
    return jnp.clip(result, min=-limit, max=limit).astype(kind)


def heavy_noise(stream_key, dims, deviation, reach, pieces, heavy, held_as=jnp.bfloat16):
    values = deviation * jax.random.normal(stream_key, dims, jnp.float32)
    if pieces:
        values = values * block_levels(stream_key, dims, pieces, -0.22, 0.18)
    return jnp.clip(with_spikes(values, jax.random.fold_in(stream_key, 3), *heavy), -reach, reach).astype(held_as)


def setup_inputs(seed: int = 0) -> dict:
    key_list = jax.random.split(jax.random.key(seed), 5)
    gradient = heavy_noise(key_list[0], (N_REPLICA, N_DP, ROWS, D), 1.0, 6.0, ((0, 4), (1, 8)), (1, 2, 8, 2.0))
    master = noise(key_list[1], (ROWS, D), D ** -0.5, 0.0625, ((0, 8), (1, 4)), jnp.float32)
    moment = noise(key_list[2], (ROWS, D), 0.003, 0.046875, ((0, 8), (1, 4)), jnp.float32)
    second = jnp.clip(jnp.exp(math.log(0.0001) - 4.6051702 * jax.random.uniform(key_list[3], (ROWS, D), jnp.float32) ** block_levels(key_list[3], (ROWS, D), ((0, 8), (1, 4)), -0.2, 0.2)), 9.999999974752427e-07, 0.0001)
    return dict(gradient=gradient, master=master, moment=moment, second=second)


def reference(gradient, master, moment, second):

    def add_block(total, block):
        return (total + lax.optimization_barrier(jnp.sum(block.astype(jnp.float32), axis=0)), None)
    start = jnp.zeros((ROWS, D), jnp.float32)
    total, unused = lax.scan(add_block, start, gradient)
    grad = total / (N_REPLICA * N_DP)
    new_moment = 0.9 * moment + 0.1 * grad
    new_second = 0.999 * second + 0.001 * grad * grad
    first_fix = 1.0 - 0.9 ** STEP
    second_fix = 1.0 - 0.999 ** STEP
    direction = new_moment / first_fix / (jnp.sqrt(new_second / second_fix) + 1e-08)
    new_master = master - 0.0003 * (direction + 0.1 * master)
    new_params = new_master.astype(jnp.bfloat16)
    dir_sq = lax.optimization_barrier(jnp.sum((direction * direction).reshape(MATS, ROWS // MATS * D), axis=1))
    wgt_sq = lax.optimization_barrier(jnp.sum((master * master).reshape(MATS, ROWS // MATS * D), axis=1))
    ratios = jnp.sqrt(dir_sq) / (jnp.sqrt(wgt_sq) + 1e-06)
    return (new_params, new_master, new_moment, new_second, direction, ratios)
```

```python
import functools

import jax
import jax.numpy as jnp
from jax import lax
from jax.experimental import pallas as pl
from jax.experimental.pallas import tpu as pltpu
from jax.sharding import PartitionSpec as P

MATS = 4
STEP = 2
LANES = 128
IDS = pl.DeviceIdType.MESH


def kernel(n_dp, n_rep, grad_hbm, master_hbm, moment_hbm, second_hbm,
           row_out, master_out, moment_out, second_out, dir_out, ratio_out,
           raw, state, tiles, rows_out, rows_in, parts, full, stats,
           load_sem, state_send, state_recv, row_send, row_recv,
           part_send, part_recv, stat_send, stat_recv):
    dp = lax.axis_index("dp")
    rep = lax.axis_index("replica")
    rows, width = raw.shape
    length = width // LANES
    block = length // n_rep

    def dp_peer(k):
        return {"dp": lax.rem(dp + k, n_dp)}

    def rep_peer(k):
        return {"replica": lax.rem(rep + k, n_rep)}

    def remote(src, dst, send, recv, peer):
        return pltpu.make_async_remote_copy(
            src_ref=src, dst_ref=dst, send_sem=send, recv_sem=recv,
            device_id=peer, device_id_type=IDS)

    own = pl.ds(pl.multiple_of(rep * block, block), block)
    grad_load = pltpu.make_async_copy(grad_hbm, raw, load_sem.at[0])
    grad_load.start()
    state_loads = [
        pltpu.make_async_copy(ref, state.at[i, own], load_sem.at[1 + i])
        for i, ref in enumerate((master_hbm, moment_hbm, second_hbm))
    ]
    for load in state_loads:
        load.start()

    barrier = pltpu.get_barrier_semaphore()
    for k in range(1, n_dp):
        pl.semaphore_signal(barrier, inc=1, device_id=dp_peer(k), device_id_type=IDS)
    for k in range(1, n_rep):
        pl.semaphore_signal(barrier, inc=1, device_id=rep_peer(k), device_id_type=IDS)

    grad_load.wait()
    for t in range(length):
        tile = raw[:, t * LANES:(t + 1) * LANES].astype(jnp.float32)
        tiles[t * rows:(t + 1) * rows, :] = tile
    pl.semaphore_wait(barrier, n_dp + n_rep - 2)

    row_copies = []
    for k in range(1, n_dp):
        peer = lax.rem(dp + k, n_dp)
        rows_out[k] = tiles[pl.ds(peer, length, stride=rows), :].astype(jnp.bfloat16)
        copy = remote(rows_out.at[k], rows_in.at[k], row_send.at[k], row_recv.at[k], dp_peer(k))
        copy.start()
        row_copies.append(copy)

    for load in state_loads:
        load.wait()
    state_copies = []
    for k in range(1, n_rep):
        copy = remote(state.at[:, own], state.at[:, own], state_send.at[k], state_recv.at[k], rep_peer(k))
        copy.start()
        state_copies.append(copy)

    total = tiles[pl.ds(dp, length, stride=rows), :]
    for k in range(1, n_dp):
        row_copies[k - 1].wait_recv()
        total = total + rows_in[k].astype(jnp.float32)
    parts[rep] = total
    part_copies = []
    for k in range(1, n_rep):
        copy = remote(parts.at[rep], parts.at[rep], part_send.at[k], part_recv.at[k], rep_peer(k))
        copy.start()
        part_copies.append(copy)

    for copy in state_copies:
        copy.wait_recv()
    for copy in part_copies:
        copy.wait_recv()
    summed = parts[0]
    for r in range(1, n_rep):
        summed = summed + parts[r]
    grad = summed / (n_dp * n_rep)
    master = state[0]
    new_moment = 0.9 * state[1] + 0.1 * grad
    new_second = 0.999 * state[2] + 0.001 * grad * grad
    first_fix = 1.0 - 0.9**STEP
    second_fix = 1.0 - 0.999**STEP
    direction = new_moment / first_fix / (jnp.sqrt(new_second / second_fix) + 1e-08)
    dir_sq = jnp.sum(direction * direction, axis=0, keepdims=True)
    wgt_sq = jnp.sum(master * master, axis=0, keepdims=True)
    stats[dp] = jnp.concatenate([dir_sq, wgt_sq], axis=0)
    stat_copies = []
    for k in range(1, n_dp):
        copy = remote(stats.at[dp], stats.at[dp], stat_send.at[k], stat_recv.at[k], dp_peer(k))
        copy.start()
        stat_copies.append(copy)

    new_master = master - 0.0003 * (direction + 0.1 * master)
    row_out[...] = new_master
    for i, value in enumerate((new_master, new_moment, new_second, direction)):
        full[i] = value
    for i, out in enumerate((master_out, moment_out, second_out, dir_out)):
        out[...] = full[i, own]

    for copy in stat_copies:
        copy.wait_recv()
    per_mat = rows // MATS
    lane = lax.broadcasted_iota(jnp.int32, (1, LANES), 1)
    ratios = jnp.zeros((1, LANES), jnp.float32)
    for m in range(MATS):
        pair = stats[m * per_mat]
        for r in range(1, per_mat):
            pair = pair + stats[m * per_mat + r]
        norms = jnp.sqrt(jnp.sum(pair, axis=1, keepdims=True))
        ratio = norms[0:1] / (norms[1:2] + 1e-06)
        ratios = jnp.where(lane == m, ratio, ratios)
    ratio_out[...] = ratios

    for copy in row_copies + state_copies + part_copies + stat_copies:
        copy.wait_send()


def local(gradient, master, moment, second):
    raw_rows = gradient[0, 0]
    rows, width = raw_rows.shape
    n_dp = lax.axis_size("dp")
    n_rep = lax.axis_size("replica")
    cols = master.shape[1]
    length, block = width // LANES, cols // LANES
    f32 = jnp.float32
    vmem = pl.BlockSpec(memory_space=pltpu.VMEM)
    dma = pltpu.SemaphoreType.DMA
    flat = [a.reshape(block, LANES) for a in (master, moment, second)]
    outs = pl.pallas_call(
        functools.partial(kernel, n_dp, n_rep),
        out_shape=[jax.ShapeDtypeStruct((length, LANES), f32)]
        + [jax.ShapeDtypeStruct((block, LANES), f32)] * 4
        + [jax.ShapeDtypeStruct((1, LANES), f32)],
        in_specs=[pl.BlockSpec(memory_space=pl.ANY)] * 4,
        out_specs=[vmem] * 6,
        scratch_shapes=[
            pltpu.VMEM((rows, width), jnp.bfloat16),
            pltpu.VMEM((3, length, LANES), f32),
            pltpu.VMEM((rows * length, LANES), f32),
            pltpu.VMEM((n_dp, length, LANES), jnp.bfloat16),
            pltpu.VMEM((n_dp, length, LANES), jnp.bfloat16),
            pltpu.VMEM((n_rep, length, LANES), f32),
            pltpu.VMEM((4, length, LANES), f32),
            pltpu.VMEM((n_dp, 2, LANES), f32),
            dma((4,)),
            dma((n_rep,)), dma((n_rep,)),
            dma((n_dp,)), dma((n_dp,)),
            dma((n_rep,)), dma((n_rep,)),
            dma((n_dp,)), dma((n_dp,)),
        ],
        compiler_params=pltpu.CompilerParams(collective_id=0, has_side_effects=True),
    )(raw_rows, *flat)
    row, new_master, new_moment, new_second, direction, ratios = outs
    new_params = row.reshape(1, width).astype(jnp.bfloat16)
    blocks = [a.reshape(1, cols) for a in (new_master, new_moment, new_second, direction)]
    return (new_params, *blocks, ratios[0, :MATS])


def solution(mesh):
    return jax.shard_map(
        local,
        mesh=mesh,
        in_specs=(
            P("replica", "dp", None, None),
            P("dp", "replica"),
            P("dp", "replica"),
            P("dp", "replica"),
        ),
        out_specs=(
            P("dp", None),
            P("dp", "replica"),
            P("dp", "replica"),
            P("dp", "replica"),
            P("dp", "replica"),
            P(),
        ),
        check_vma=False,
    )
```

```python
import functools

import jax
import jax.numpy as jnp
from jax import lax
from jax.experimental import pallas as pl
from jax.experimental.pallas import tpu as pltpu
from jax.sharding import PartitionSpec as P

MATS = 4
STEP = 2
LANES = 128
IDS = pl.DeviceIdType.MESH


def kernel(n_dp, n_rep, grad_hbm, master_hbm, moment_hbm, second_hbm,
           row_out, blocks_out, ratio_out,
           raw, state, tiles, rows_out, rows_in, parts, full, stats,
           load_sem, state_send, state_recv, row_send, row_recv,
           part_send, part_recv, stat_send, stat_recv):
    dp = lax.axis_index("dp")
    rep = lax.axis_index("replica")
    rows, width = raw.shape
    length = width // LANES
    block = length // n_rep

    def dp_peer(k):
        return {"dp": lax.rem(dp + k, n_dp)}

    def rep_peer(k):
        return {"replica": lax.rem(rep + k, n_rep)}

    def remote(src, dst, send, recv, peer):
        return pltpu.make_async_remote_copy(
            src_ref=src, dst_ref=dst, send_sem=send, recv_sem=recv,
            device_id=peer, device_id_type=IDS)

    own = pl.ds(pl.multiple_of(rep * block, block), block)
    grad_load = pltpu.make_async_copy(grad_hbm, raw, load_sem.at[0])
    grad_load.start()
    state_loads = [
        pltpu.make_async_copy(ref, state.at[i, own], load_sem.at[1 + i])
        for i, ref in enumerate((master_hbm, moment_hbm, second_hbm))
    ]
    for load in state_loads:
        load.start()

    barrier = pltpu.get_barrier_semaphore()
    for k in range(1, n_dp):
        pl.semaphore_signal(barrier, inc=1, device_id=dp_peer(k), device_id_type=IDS)
    for k in range(1, n_rep):
        pl.semaphore_signal(barrier, inc=1, device_id=rep_peer(k), device_id_type=IDS)

    grad_load.wait()
    for t in range(length):
        tile = raw[:, t * LANES:(t + 1) * LANES].astype(jnp.float32)
        tiles[t * rows:(t + 1) * rows, :] = tile
    pl.semaphore_wait(barrier, n_dp + n_rep - 2)

    row_copies = []
    for k in range(1, n_dp):
        peer = lax.rem(dp + k, n_dp)
        rows_out[k] = tiles[pl.ds(peer, length, stride=rows), :].astype(jnp.bfloat16)
        copy = remote(rows_out.at[k], rows_in.at[k], row_send.at[k], row_recv.at[k], dp_peer(k))
        copy.start()
        row_copies.append(copy)

    for load in state_loads:
        load.wait()
    state_copies = []
    for k in range(1, n_rep):
        copy = remote(state.at[:, own], state.at[:, own], state_send.at[k], state_recv.at[k], rep_peer(k))
        copy.start()
        state_copies.append(copy)

    total = tiles[pl.ds(dp, length, stride=rows), :]
    for k in range(1, n_dp):
        row_copies[k - 1].wait_recv()
        total = total + rows_in[k].astype(jnp.float32)
    parts[rep] = total
    part_copies = []
    for k in range(1, n_rep):
        copy = remote(parts.at[rep], parts.at[rep], part_send.at[k], part_recv.at[k], rep_peer(k))
        copy.start()
        part_copies.append(copy)

    for copy in state_copies:
        copy.wait_recv()
    for copy in part_copies:
        copy.wait_recv()
    summed = parts[0]
    for r in range(1, n_rep):
        summed = summed + parts[r]
    grad = summed / (n_dp * n_rep)
    master = state[0]
    new_moment = 0.9 * state[1] + 0.1 * grad
    new_second = 0.999 * state[2] + 0.001 * grad * grad
    first_fix = 1.0 - 0.9**STEP
    second_fix = 1.0 - 0.999**STEP
    direction = new_moment / first_fix / (jnp.sqrt(new_second / second_fix) + 1e-08)
    dir_sq = jnp.sum(direction * direction, axis=0, keepdims=True)
    wgt_sq = jnp.sum(master * master, axis=0, keepdims=True)
    stats[dp] = jnp.concatenate([dir_sq, wgt_sq], axis=0)
    stat_copies = []
    for k in range(1, n_dp):
        copy = remote(stats.at[dp], stats.at[dp], stat_send.at[k], stat_recv.at[k], dp_peer(k))
        copy.start()
        stat_copies.append(copy)

    new_master = master - 0.0003 * (direction + 0.1 * master)
    row_out[...] = new_master
    for i, value in enumerate((new_master, new_moment, new_second, direction)):
        full[i] = value
    for i in range(4):
        blocks_out[i] = full[i, own]

    for copy in stat_copies:
        copy.wait_recv()
    per_mat = rows // MATS
    lane = lax.broadcasted_iota(jnp.int32, (1, LANES), 1)
    ratios = jnp.zeros((1, LANES), jnp.float32)
    for m in range(MATS):
        pair = stats[m * per_mat]
        for r in range(1, per_mat):
            pair = pair + stats[m * per_mat + r]
        norms = jnp.sqrt(jnp.sum(pair, axis=1, keepdims=True))
        ratio = norms[0:1] / (norms[1:2] + 1e-06)
        ratios = jnp.where(lane == m, ratio, ratios)
    ratio_out[...] = ratios

    for copy in row_copies + state_copies + part_copies + stat_copies:
        copy.wait_send()


def finish(row_ref, blocks_ref, ratio_ref, params_out, master_out, moment_out, second_out, dir_out, ratio_out):
    for t in range(row_ref.shape[0]):
        params_out[:, t * LANES:(t + 1) * LANES] = row_ref[t:t + 1, :].astype(jnp.bfloat16)
    for i, out in enumerate((master_out, moment_out, second_out, dir_out)):
        out[...] = blocks_ref[i]
    ratio_out[...] = ratio_ref[0, :MATS]


def local(gradient, master, moment, second):
    raw_rows = gradient[0, 0]
    rows, width = raw_rows.shape
    n_dp = lax.axis_size("dp")
    n_rep = lax.axis_size("replica")
    cols = master.shape[1]
    length, block = width // LANES, cols // LANES
    f32 = jnp.float32
    vmem = pl.BlockSpec(memory_space=pltpu.VMEM)
    dma = pltpu.SemaphoreType.DMA
    flat = [a.reshape(block, LANES) for a in (master, moment, second)]
    row, blocks, ratios = pl.pallas_call(
        functools.partial(kernel, n_dp, n_rep),
        out_shape=[
            pltpu.VMEM((length, LANES), f32),
            pltpu.VMEM((4, block, LANES), f32),
            pltpu.VMEM((1, LANES), f32),
        ],
        in_specs=[pl.BlockSpec(memory_space=pl.ANY)] * 4,
        out_specs=[vmem] * 3,
        scratch_shapes=[
            pltpu.VMEM((rows, width), jnp.bfloat16),
            pltpu.VMEM((3, length, LANES), f32),
            pltpu.VMEM((rows * length, LANES), f32),
            pltpu.VMEM((n_dp, length, LANES), jnp.bfloat16),
            pltpu.VMEM((n_dp, length, LANES), jnp.bfloat16),
            pltpu.VMEM((n_rep, length, LANES), f32),
            pltpu.VMEM((4, length, LANES), f32),
            pltpu.VMEM((n_dp, 2, LANES), f32),
            dma((4,)),
            dma((n_rep,)), dma((n_rep,)),
            dma((n_dp,)), dma((n_dp,)),
            dma((n_rep,)), dma((n_rep,)),
            dma((n_dp,)), dma((n_dp,)),
        ],
        compiler_params=pltpu.CompilerParams(collective_id=0, has_side_effects=True),
    )(raw_rows, *flat)
    row, blocks, ratios = (
        pltpu.with_memory_space_constraint(a, pltpu.VMEM) for a in (row, blocks, ratios))
    outs = pl.pallas_call(
        finish,
        out_shape=[jax.ShapeDtypeStruct((1, width), jnp.bfloat16)]
        + [jax.ShapeDtypeStruct((block, LANES), f32)] * 4
        + [jax.ShapeDtypeStruct((MATS,), f32)],
        in_specs=[vmem] * 3,
        out_specs=[vmem] * 6,
    )(row, blocks, ratios)
    new_params, new_master, new_moment, new_second, direction, ratios = outs
    new_blocks = [a.reshape(1, cols) for a in (new_master, new_moment, new_second, direction)]
    return (new_params, *new_blocks, ratios)


def solution(mesh):
    return jax.shard_map(
        local,
        mesh=mesh,
        in_specs=(
            P("replica", "dp", None, None),
            P("dp", "replica"),
            P("dp", "replica"),
            P("dp", "replica"),
        ),
        out_specs=(
            P("dp", None),
            P("dp", "replica"),
            P("dp", "replica"),
            P("dp", "replica"),
            P("dp", "replica"),
            P(),
        ),
        check_vma=False,
    )
```

```python
import functools

import jax
import jax.numpy as jnp
from jax import lax
from jax.experimental import pallas as pl
from jax.experimental.pallas import tpu as pltpu
from jax.sharding import PartitionSpec as P

MATS = 4
STEP = 2
LANES = 128
IDS = pl.DeviceIdType.MESH


def staged(n_dp, n_rep, grad_hbm, master_hbm, moment_hbm, second_hbm,
           row_out, blocks_out, ratio_out,
           raw, state, tiles, rows_out, rows_in, parts, full, stats,
           load_sem, state_send, state_recv, row_send, row_recv,
           part_send, part_recv, stat_send, stat_recv):
    dp = lax.axis_index("dp")
    rep = lax.axis_index("replica")
    rows, width = raw.shape
    length = width // LANES
    block = length // n_rep

    def dp_peer(k):
        return {"dp": lax.rem(dp + k, n_dp)}

    def rep_peer(k):
        return {"replica": lax.rem(rep + k, n_rep)}

    def remote(src, dst, send, recv, peer):
        return pltpu.make_async_remote_copy(
            src_ref=src, dst_ref=dst, send_sem=send, recv_sem=recv,
            device_id=peer, device_id_type=IDS)

    own = pl.ds(pl.multiple_of(rep * block, block), block)
    grad_load = pltpu.make_async_copy(grad_hbm, raw, load_sem.at[0])
    grad_load.start()
    state_loads = [
        pltpu.make_async_copy(ref, state.at[i, own], load_sem.at[1 + i])
        for i, ref in enumerate((master_hbm, moment_hbm, second_hbm))
    ]
    for load in state_loads:
        load.start()

    barrier = pltpu.get_barrier_semaphore()
    for k in range(1, n_dp):
        pl.semaphore_signal(barrier, inc=1, device_id=dp_peer(k), device_id_type=IDS)
    for k in range(1, n_rep):
        pl.semaphore_signal(barrier, inc=1, device_id=rep_peer(k), device_id_type=IDS)

    grad_load.wait()
    for t in range(length):
        tile = raw[:, t * LANES:(t + 1) * LANES].astype(jnp.float32)
        tiles[t * rows:(t + 1) * rows, :] = tile
    pl.semaphore_wait(barrier, n_dp + n_rep - 2)

    row_copies = []
    for k in range(1, n_dp):
        peer = lax.rem(dp + k, n_dp)
        rows_out[k] = tiles[pl.ds(peer, length, stride=rows), :].astype(jnp.bfloat16)
        copy = remote(rows_out.at[k], rows_in.at[k], row_send.at[k], row_recv.at[k], dp_peer(k))
        copy.start()
        row_copies.append(copy)

    for load in state_loads:
        load.wait()
    state_copies = []
    for k in range(1, n_rep):
        copy = remote(state.at[:, own], state.at[:, own], state_send.at[k], state_recv.at[k], rep_peer(k))
        copy.start()
        state_copies.append(copy)

    total = tiles[pl.ds(dp, length, stride=rows), :]
    for k in range(1, n_dp):
        row_copies[k - 1].wait_recv()
        total = total + rows_in[k].astype(jnp.float32)
    parts[rep] = total
    part_copies = []
    for k in range(1, n_rep):
        copy = remote(parts.at[rep], parts.at[rep], part_send.at[k], part_recv.at[k], rep_peer(k))
        copy.start()
        part_copies.append(copy)

    for copy in state_copies:
        copy.wait_recv()
    for copy in part_copies:
        copy.wait_recv()
    summed = parts[0]
    for r in range(1, n_rep):
        summed = summed + parts[r]
    grad = summed / (n_dp * n_rep)
    master = state[0]
    new_moment = 0.9 * state[1] + 0.1 * grad
    new_second = 0.999 * state[2] + 0.001 * grad * grad
    first_fix = 1.0 - 0.9**STEP
    second_fix = 1.0 - 0.999**STEP
    direction = new_moment / first_fix / (jnp.sqrt(new_second / second_fix) + 1e-08)
    dir_sq = jnp.sum(direction * direction, axis=0, keepdims=True)
    wgt_sq = jnp.sum(master * master, axis=0, keepdims=True)
    stats[dp] = jnp.concatenate([dir_sq, wgt_sq], axis=0)
    stat_copies = []
    for k in range(1, n_dp):
        copy = remote(stats.at[dp], stats.at[dp], stat_send.at[k], stat_recv.at[k], dp_peer(k))
        copy.start()
        stat_copies.append(copy)

    new_master = master - 0.0003 * (direction + 0.1 * master)
    row_out[...] = new_master
    for i, value in enumerate((new_master, new_moment, new_second, direction)):
        full[i] = value
    for i in range(4):
        blocks_out[i] = full[i, own]

    for copy in stat_copies:
        copy.wait_recv()
    per_mat = rows // MATS
    lane = lax.broadcasted_iota(jnp.int32, (1, LANES), 1)
    ratios = jnp.zeros((1, LANES), jnp.float32)
    for m in range(MATS):
        pair = stats[m * per_mat]
        for r in range(1, per_mat):
            pair = pair + stats[m * per_mat + r]
        norms = jnp.sqrt(jnp.sum(pair, axis=1, keepdims=True))
        ratio = norms[0:1] / (norms[1:2] + 1e-06)
        ratios = jnp.where(lane == m, ratio, ratios)
    ratio_out[...] = ratios

    for copy in row_copies + state_copies + part_copies + stat_copies:
        copy.wait_send()


def direct(n_dp, n_rep, grad_hbm, master_hbm, moment_hbm, second_hbm,
           row_out, blocks_out, ratio_out,
           raw, state, tiles, outgoing, incoming, params, stat, stats,
           load_sem, row_send, row_recv, param_send, param_recv, stat_send, stat_recv):
    dp = lax.axis_index("dp")
    rep = lax.axis_index("replica")
    rows, cols = raw.shape[1:]
    block = cols // LANES
    peers = [(j, k) for j in list(range(1, n_rep)) + [0] for k in range(n_dp) if j or k]
    count = len(peers)

    def at(j, k):
        return {"dp": lax.rem(dp + k, n_dp), "replica": lax.rem(rep + j, n_rep)}

    def remote(src, dst, send, recv, peer):
        return pltpu.make_async_remote_copy(
            src_ref=src, dst_ref=dst, send_sem=send, recv_sem=recv,
            device_id=peer, device_id_type=IDS)

    loads = {}
    for j in list(range(1, n_rep)) + [0]:
        first = pl.multiple_of(lax.rem(rep + j, n_rep) * cols, cols)
        loads[j] = pltpu.make_async_copy(grad_hbm.at[:, pl.ds(first, cols)], raw.at[j], load_sem.at[j])
        loads[j].start()
    state_loads = [
        pltpu.make_async_copy(ref, state.at[i], load_sem.at[n_rep + i])
        for i, ref in enumerate((master_hbm, moment_hbm, second_hbm))
    ]
    for load in state_loads:
        load.start()

    barrier = pltpu.get_barrier_semaphore()
    for j, k in peers:
        pl.semaphore_signal(barrier, inc=1, device_id=at(j, k), device_id_type=IDS)

    slot = 0
    row_copies = []
    for j in list(range(1, n_rep)) + [0]:
        loads[j].wait()
        for t in range(block):
            tile = raw[j, :, t * LANES:(t + 1) * LANES].astype(jnp.float32)
            tiles[j, t * rows:(t + 1) * rows, :] = tile
        if slot == 0:
            pl.semaphore_wait(barrier, count)
        for k in range(n_dp):
            if j == 0 and k == 0:
                continue
            target = lax.rem(dp + k, n_dp)
            outgoing[slot] = tiles[j, pl.ds(target, block, stride=rows), :].astype(jnp.bfloat16)
            copy = remote(outgoing.at[slot], incoming.at[slot], row_send.at[slot], row_recv.at[slot], at(j, k))
            copy.start()
            row_copies.append(copy)
            slot += 1

    for load in state_loads:
        load.wait()
    master = state[0]
    wgt_sq = jnp.sum(master * master, axis=0, keepdims=True)
    stat[1:2] = wgt_sq
    total = tiles[0, pl.ds(dp, block, stride=rows), :]
    for s in range(count):
        row_copies[s].wait_recv()
        total = total + incoming[s].astype(jnp.float32)
    grad = total * (1.0 / (n_dp * n_rep))
    new_moment = 0.9 * state[1] + 0.1 * grad
    new_second = 0.999 * state[2] + 0.001 * grad * grad
    first_scale = 1.0 / (1.0 - 0.9**STEP)
    second_scale = 1.0 / (1.0 - 0.999**STEP)
    direction = new_moment * first_scale / (jnp.sqrt(new_second * second_scale) + 1e-08)
    new_master = master - 0.0003 * (direction + 0.1 * master)

    stat[0:1] = jnp.sum(direction * direction, axis=0, keepdims=True)
    mine = dp * n_rep + rep
    stat_copies = []
    for s, (j, k) in enumerate(peers):
        copy = remote(stat, stats.at[mine], stat_send.at[s], stat_recv.at[s], at(j, k))
        copy.start()
        stat_copies.append(copy)
    params[rep] = new_master.astype(jnp.bfloat16)
    param_copies = []
    for j in range(1, n_rep):
        copy = remote(params.at[rep], params.at[rep], param_send.at[j], param_recv.at[j], at(j, 0))
        copy.start()
        param_copies.append(copy)

    stats[mine] = stat[...]
    for i, value in enumerate((new_master, new_moment, new_second, direction)):
        blocks_out[i] = value
    for copy in row_copies:
        copy.wait_send()

    for copy in param_copies:
        copy.wait_recv()
    for r in range(n_rep):
        row_out[r * block:(r + 1) * block, :] = params[r].astype(jnp.float32)
    for copy in stat_copies:
        copy.wait_recv()
    per_mat = n_dp * n_rep // MATS
    lane = lax.broadcasted_iota(jnp.int32, (1, LANES), 1)
    ratios = jnp.zeros((1, LANES), jnp.float32)
    for m in range(MATS):
        pair = stats[m * per_mat]
        for r in range(1, per_mat):
            pair = pair + stats[m * per_mat + r]
        norms = jnp.sqrt(jnp.sum(pair, axis=1, keepdims=True))
        ratio = norms[0:1] / (norms[1:2] + 1e-06)
        ratios = jnp.where(lane == m, ratio, ratios)
    ratio_out[...] = ratios
    for copy in param_copies + stat_copies:
        copy.wait_send()


def finish(row_ref, blocks_ref, ratio_ref, params_out, master_out, moment_out, second_out, dir_out, ratio_out):
    for t in range(row_ref.shape[0]):
        params_out[:, t * LANES:(t + 1) * LANES] = row_ref[t:t + 1, :].astype(jnp.bfloat16)
    for i, out in enumerate((master_out, moment_out, second_out, dir_out)):
        out[...] = blocks_ref[i]
    ratio_out[...] = ratio_ref[0, :MATS]


def local(gradient, master, moment, second):
    raw_rows = gradient[0, 0]
    rows, width = raw_rows.shape
    n_dp = lax.axis_size("dp")
    n_rep = lax.axis_size("replica")
    cols = master.shape[1]
    length, block = width // LANES, cols // LANES
    f32 = jnp.float32
    vmem = pl.BlockSpec(memory_space=pltpu.VMEM)
    dma = pltpu.SemaphoreType.DMA
    flat = [a.reshape(block, LANES) for a in (master, moment, second)]
    count = n_dp * n_rep
    if count <= 64:
        body = direct
        scratch = [
            pltpu.VMEM((n_rep, rows, cols), jnp.bfloat16),
            pltpu.VMEM((3, block, LANES), f32),
            pltpu.VMEM((n_rep, rows * block, LANES), f32),
            pltpu.VMEM((count - 1, block, LANES), jnp.bfloat16),
            pltpu.VMEM((count - 1, block, LANES), jnp.bfloat16),
            pltpu.VMEM((n_rep, block, LANES), jnp.bfloat16),
            pltpu.VMEM((2, LANES), f32),
            pltpu.VMEM((count, 2, LANES), f32),
            dma((n_rep + 3,)),
            dma((count - 1,)), dma((count - 1,)),
            dma((n_rep,)), dma((n_rep,)),
            dma((count - 1,)), dma((count - 1,)),
        ]
    else:
        body = staged
        scratch = [
            pltpu.VMEM((rows, width), jnp.bfloat16),
            pltpu.VMEM((3, length, LANES), f32),
            pltpu.VMEM((rows * length, LANES), f32),
            pltpu.VMEM((n_dp, length, LANES), jnp.bfloat16),
            pltpu.VMEM((n_dp, length, LANES), jnp.bfloat16),
            pltpu.VMEM((n_rep, length, LANES), f32),
            pltpu.VMEM((4, length, LANES), f32),
            pltpu.VMEM((n_dp, 2, LANES), f32),
            dma((4,)),
            dma((n_rep,)), dma((n_rep,)),
            dma((n_dp,)), dma((n_dp,)),
            dma((n_rep,)), dma((n_rep,)),
            dma((n_dp,)), dma((n_dp,)),
        ]
    row, blocks, ratios = pl.pallas_call(
        functools.partial(body, n_dp, n_rep),
        out_shape=[
            pltpu.VMEM((length, LANES), f32),
            pltpu.VMEM((4, block, LANES), f32),
            pltpu.VMEM((1, LANES), f32),
        ],
        in_specs=[pl.BlockSpec(memory_space=pl.ANY)] * 4,
        out_specs=[vmem] * 3,
        scratch_shapes=scratch,
        compiler_params=pltpu.CompilerParams(collective_id=0, has_side_effects=True),
    )(raw_rows, *flat)
    row, blocks, ratios = (
        pltpu.with_memory_space_constraint(a, pltpu.VMEM) for a in (row, blocks, ratios))
    outs = pl.pallas_call(
        finish,
        out_shape=[jax.ShapeDtypeStruct((1, width), jnp.bfloat16)]
        + [jax.ShapeDtypeStruct((block, LANES), f32)] * 4
        + [jax.ShapeDtypeStruct((MATS,), f32)],
        in_specs=[vmem] * 3,
        out_specs=[vmem] * 6,
    )(row, blocks, ratios)
    new_params, new_master, new_moment, new_second, direction, ratios = outs
    new_blocks = [a.reshape(1, cols) for a in (new_master, new_moment, new_second, direction)]
    return (new_params, *new_blocks, ratios)


def solution(mesh):
    return jax.shard_map(
        local,
        mesh=mesh,
        in_specs=(
            P("replica", "dp", None, None),
            P("dp", "replica"),
            P("dp", "replica"),
            P("dp", "replica"),
        ),
        out_specs=(
            P("dp", None),
            P("dp", "replica"),
            P("dp", "replica"),
            P("dp", "replica"),
            P("dp", "replica"),
            P(),
        ),
        check_vma=False,
    )
```

```python
import functools

import jax
import jax.numpy as jnp
from jax import lax
from jax.experimental import pallas as pl
from jax.experimental.pallas import tpu as pltpu
from jax.sharding import PartitionSpec as P

MATS = 4
STEP = 2
LANES = 128
IDS = pl.DeviceIdType.MESH


def kernel(n_dp, n_rep, grad_hbm, master_hbm, moment_hbm, second_hbm,
           row_out, blocks_out, ratio_out,
           raw, state, tiles, rows_out, rows_in, parts, full, stats,
           load_sem, state_send, state_recv, row_send, row_recv,
           part_send, part_recv, stat_send, stat_recv):
    dp = lax.axis_index("dp")
    rep = lax.axis_index("replica")
    rows, width = raw.shape
    length = width // LANES
    block = length // n_rep

    def dp_peer(k):
        return {"dp": lax.rem(dp + k, n_dp)}

    def rep_peer(k):
        return {"replica": lax.rem(rep + k, n_rep)}

    def remote(src, dst, send, recv, peer):
        return pltpu.make_async_remote_copy(
            src_ref=src, dst_ref=dst, send_sem=send, recv_sem=recv,
            device_id=peer, device_id_type=IDS)

    def settle(ref, sem):
        pltpu.make_async_copy(ref, ref, sem.at[0]).wait()

    own = pl.ds(pl.multiple_of(rep * block, block), block)
    offsets = sorted(range(1, n_dp), key=lambda k: abs(2 * k - n_dp))
    grad_load = pltpu.make_async_copy(grad_hbm, raw, load_sem.at[0])
    grad_load.start()

    barrier = pltpu.get_barrier_semaphore()
    for k in offsets:
        pl.semaphore_signal(barrier, inc=1, device_id=dp_peer(k), device_id_type=IDS)
    for k in range(1, n_rep):
        pl.semaphore_signal(barrier, inc=1, device_id=rep_peer(k), device_id_type=IDS)

    state_loads = [
        pltpu.make_async_copy(ref, state.at[i, own], load_sem.at[1 + i])
        for i, ref in enumerate((master_hbm, moment_hbm, second_hbm))
    ]
    for load in state_loads:
        load.start()
    grad_load.wait()
    for t in range(length):
        tile = raw[:, t * LANES:(t + 1) * LANES].astype(jnp.float32)
        tiles[t * rows:(t + 1) * rows, :] = tile
    for k in offsets:
        peer = lax.rem(dp + k, n_dp)
        rows_out[k] = tiles[pl.ds(peer, length, stride=rows), :].astype(jnp.bfloat16)
    for load in state_loads:
        load.wait()
    pl.semaphore_wait(barrier, n_dp + n_rep - 2)

    for k in offsets:
        copy = remote(rows_out.at[k], rows_in.at[k], row_send.at[0], row_recv.at[0], dp_peer(k))
        copy.start()
    for k in range(1, n_rep):
        copy = remote(state.at[:, own], state.at[:, own], state_send.at[0], state_recv.at[0], rep_peer(k))
        copy.start()

    total = tiles[pl.ds(dp, length, stride=rows), :]
    settle(rows_in.at[1:n_dp], row_recv)
    for k in offsets:
        total = total + rows_in[k].astype(jnp.float32)
    parts[rep] = total
    for k in range(1, n_rep):
        copy = remote(parts.at[rep], parts.at[rep], part_send.at[0], part_recv.at[0], rep_peer(k))
        copy.start()

    settle(state.at[:, 0:(n_rep - 1) * block], state_recv)
    master = state[0]
    stats[dp, 1:2] = jnp.sum(master * master, axis=0, keepdims=True)
    old_moment = 0.9 * state[1]
    old_second = 0.999 * state[2]
    settle(rows_out.at[1:n_dp], row_send)
    settle(state.at[:, 0:(n_rep - 1) * block], state_send)
    settle(parts.at[1:n_rep], part_recv)
    summed = parts[0]
    for r in range(1, n_rep):
        summed = summed + parts[r]
    grad = summed * (1.0 / (n_dp * n_rep))
    new_moment = old_moment + 0.1 * grad
    new_second = old_second + 0.001 * grad * grad
    first_scale = 1.0 / (1.0 - 0.9**STEP)
    second_scale = 1.0 / (1.0 - 0.999**STEP)
    direction = new_moment * first_scale / (jnp.sqrt(new_second * second_scale) + 1e-08)
    stats[dp, 0:1] = jnp.sum(direction * direction, axis=0, keepdims=True)
    for k in offsets:
        copy = remote(stats.at[dp], stats.at[dp], stat_send.at[0], stat_recv.at[0], dp_peer(k))
        copy.start()

    new_master = master - 0.0003 * (direction + 0.1 * master)
    row_out[...] = new_master
    for i, value in enumerate((new_master, new_moment, new_second, direction)):
        full[i] = value
    for i in range(4):
        blocks_out[i] = full[i, own]
    settle(parts.at[1:n_rep], part_send)

    settle(stats.at[1:n_dp], stat_recv)
    per_mat = rows // MATS
    lane = lax.broadcasted_iota(jnp.int32, (1, LANES), 1)
    ratios = jnp.zeros((1, LANES), jnp.float32)
    for m in range(MATS):
        pair = stats[m * per_mat]
        for r in range(1, per_mat):
            pair = pair + stats[m * per_mat + r]
        norms = jnp.sqrt(jnp.sum(pair, axis=1, keepdims=True))
        ratio = norms[0:1] / (norms[1:2] + 1e-06)
        ratios = jnp.where(lane == m, ratio, ratios)
    ratio_out[...] = ratios

    settle(stats.at[1:n_dp], stat_send)


def finish(row_ref, blocks_ref, ratio_ref, params_out, master_out, moment_out, second_out, dir_out, ratio_out):
    for t in range(row_ref.shape[0]):
        params_out[:, t * LANES:(t + 1) * LANES] = row_ref[t:t + 1, :].astype(jnp.bfloat16)
    for i, out in enumerate((master_out, moment_out, second_out, dir_out)):
        out[...] = blocks_ref[i]
    ratio_out[...] = ratio_ref[0, :MATS]


def local(gradient, master, moment, second):
    raw_rows = gradient[0, 0]
    rows, width = raw_rows.shape
    n_dp = lax.axis_size("dp")
    n_rep = lax.axis_size("replica")
    cols = master.shape[1]
    length, block = width // LANES, cols // LANES
    f32 = jnp.float32
    vmem = pl.BlockSpec(memory_space=pltpu.VMEM)
    dma = pltpu.SemaphoreType.DMA
    flat = [a.reshape(block, LANES) for a in (master, moment, second)]
    row, blocks, ratios = pl.pallas_call(
        functools.partial(kernel, n_dp, n_rep),
        out_shape=[
            pltpu.VMEM((length, LANES), f32),
            pltpu.VMEM((4, block, LANES), f32),
            pltpu.VMEM((1, LANES), f32),
        ],
        in_specs=[pl.BlockSpec(memory_space=pl.ANY)] * 4,
        out_specs=[vmem] * 3,
        scratch_shapes=[
            pltpu.VMEM((rows, width), jnp.bfloat16),
            pltpu.VMEM((3, length, LANES), f32),
            pltpu.VMEM((rows * length, LANES), f32),
            pltpu.VMEM((n_dp, length, LANES), jnp.bfloat16),
            pltpu.VMEM((n_dp, length, LANES), jnp.bfloat16),
            pltpu.VMEM((n_rep, length, LANES), f32),
            pltpu.VMEM((4, length, LANES), f32),
            pltpu.VMEM((n_dp, 2, LANES), f32),
            dma((4,)),
            *[dma((1,))] * 8,
        ],
        compiler_params=pltpu.CompilerParams(collective_id=0, has_side_effects=True),
    )(raw_rows, *flat)
    row, blocks, ratios = (
        pltpu.with_memory_space_constraint(a, pltpu.VMEM) for a in (row, blocks, ratios))
    outs = pl.pallas_call(
        finish,
        out_shape=[jax.ShapeDtypeStruct((1, width), jnp.bfloat16)]
        + [jax.ShapeDtypeStruct((block, LANES), f32)] * 4
        + [jax.ShapeDtypeStruct((MATS,), f32)],
        in_specs=[vmem] * 3,
        out_specs=[vmem] * 6,
    )(row, blocks, ratios)
    new_params, new_master, new_moment, new_second, direction, ratios = outs
    new_blocks = [a.reshape(1, cols) for a in (new_master, new_moment, new_second, direction)]
    return (new_params, *new_blocks, ratios)


def solution(mesh):
    return jax.shard_map(
        local,
        mesh=mesh,
        in_specs=(
            P("replica", "dp", None, None),
            P("dp", "replica"),
            P("dp", "replica"),
            P("dp", "replica"),
        ),
        out_specs=(
            P("dp", None),
            P("dp", "replica"),
            P("dp", "replica"),
            P("dp", "replica"),
            P("dp", "replica"),
            P(),
        ),
        check_vma=False,
    )
```
